32 devices in a mesh: section: 2 (over core), ctx: 4 (over z), mp: 4 (over y, x).
Axes of the slice: x: 2, y: 2, z: 4, core: 2. Of those that a mesh axis runs over, the one named last changes fastest.
Arguments:
- frames: bfloat16 [2, 16, 128, 512], P('section', 'ctx'), may hold values from -6 to 6
- w_conv: bfloat16 [3, 512, 512], replicated, may hold values from -0.15625 to 0.15625
- w_lat: bfloat16 [512, 16], replicated, may hold values from -0.25 to 0.25
- dest: int32 [2, 512, 1], P(None, 'ctx'), may hold values from 0 to 3; in each aligned block of 128 rows (0 to 127, 128 to 255, ..., all dimensions but the last counted through in order) at most 48 rows name the same one
- pick: int32 [2, 512], P(None, 'ctx'), may hold values from 0 to 6
- w_embed: bfloat16 [64, 6144], replicated, may hold values from -0.75 to 0.75
- gain: float32 [6144], replicated, may hold values from 0.25 to 1.75
- w_qkv: bfloat16 [6144, 3, 4096], P(None, None, 'mp'), may hold values from -0.078125 to 0.078125
Outputs:
- attended: bfloat16 [2, 768, 4096], P('section', 'ctx', 'mp')
The draws below stay inside these ranges and needn't reach their ends.
Inputs may be any that keep to these rules, and one draw needn't show every extreme that they name: `dest`: among the 128 rows of one frame block, at most 48 name the same context shard, and some frame block reaches 48.
All inputs are finite; a program needn't handle non-finite values.
Results may differ from the reference program's by a relative error of at most 0.0061.
Values may be sent and summed in bfloat16 or wider, within the bound.
A program may use at most 128 MiB of HBM per device.

```python
import math
import jax
import jax.numpy as jnp
import numpy as np
from jax import lax

D = 6144
HEAD = 128
HEADS = 32
C_ENC = 512
LATC = 16
LATENT = 64
FRAMES = 4
CELLS = 128
GROUP = 4
ROWS = 128
NGROUP = 1
CAP = 48
TOKENS = 512
N_CTX = 4


def set_ends(values, own_key, least, high):
    longest = values.shape.index(max(values.shape))
    spots = []
    for shift in (0, 1):
        where = [jax.random.randint(jax.random.fold_in(own_key, axis), (), 0, length) for axis, length in enumerate(values.shape)]
        where[longest] = (where[longest] + shift) % values.shape[longest]
        spots.append(tuple(where))
    return values.at[spots[0]].set(least).at[spots[1]].set(high)


def level_of(stream_key, dims, pieces, smallest, top_value):
    level = 1.0
    for dim, parts in pieces:
        steps = jax.random.uniform(jax.random.fold_in(jax.random.fold_in(stream_key, 6), dim), (parts,), jnp.float32, smallest / len(pieces), top_value / len(pieces))
        level = level * jnp.repeat(jnp.exp(steps), dims[dim] // parts).reshape((-1,) + (1,) * (len(dims) - 1 - dim))
    return level


def assign_block(key, own, number, rows, number_of, top, limit, skew):
    order = jax.random.permutation(key, number_of)
    packed, ordinary = shares(number_of, rows * top, limit, skew, True), shares(number_of, rows * top, limit, skew, False)
    places = jnp.arange(number_of)

    def named(tallies, offset_by):
        used = int((tallies > 0).sum())
        fixed = max(1, used // 4)
        moved = fixed + (places - fixed + offset_by * (used - fixed)) % max(1, number_of - fixed)
        return jnp.zeros((number_of,), jnp.int32).at[order[jnp.where(places < fixed, places, moved)]].set(jnp.asarray(tallies, jnp.int32))

    tallies = jnp.where(number % 4 == 0, named(packed, number // 4), named(ordinary, number - number // 4 - 1))
    mixed = jax.random.permutation(jax.random.fold_in(own, 3), number_of)
    donor, sink = mixed[0:number_of // 2 * 2:2], mixed[1:number_of // 2 * 2:2]
    room = jnp.minimum(tallies[donor] - 1, limit - tallies[sink]) // 2
    room = jnp.where((donor == order[0]) | (sink == order[0]) | (tallies[sink] == 0), 0, jnp.maximum(room, 0))
    moved = jax.random.randint(jax.random.fold_in(own, 4), (number_of // 2,), 0, 1 << 20) % (room + 1)
    tallies = tallies.at[donor].add(-moved).at[sink].add(moved)
    members = jnp.searchsorted(jnp.cumsum(tallies), jnp.arange(rows * top), side="right").astype(jnp.int32)
    grid = members.reshape(top, rows).T
    grid = grid[jax.random.permutation(jax.random.fold_in(own, 1), rows)]
    offset_by = jax.random.randint(jax.random.fold_in(own, 2), (rows, 1), 0, top)
    return jnp.take_along_axis(grid, (jnp.arange(top)[None, :] + offset_by) % top, axis=1)


def shares(count, total, most, slope, full):
    loads = [(1 << 20) // math.isqrt(standing ** slope) + 1 for standing in range(1, count + 1)]
    largest = most if full else min(most, max(-(-total // count), total * loads[0] // sum(loads)))
    least = 1 if total - largest >= count - 1 else 0
    counts, spare = [largest] + [least] * (count - 1), total - largest - least * (count - 1)
    while spare > 0:
        movable = [i for i in range(1, count) if counts[i] < largest] or [i for i in range(1, count) if counts[i] < most]
        whole, budget = sum([loads[i] for i in movable]), spare
        for i in movable:
            extra = min(most - counts[i], max(1, budget * loads[i] // whole), spare)
            counts[i] = counts[i] + extra
            spare = spare - extra
    return np.array(counts)


def gaussian(rng, extent, spread, bound, pieces=(), held_as=jnp.bfloat16):
    array = spread * jax.random.normal(rng, extent, jnp.float32)
    if pieces:
        array = array * level_of(rng, extent, pieces, -0.22, 0.18)
    return jnp.clip(array, -bound, bound).astype(held_as)


def setup_inputs(seed: int = 0) -> dict:
    splits = jax.random.split(jax.random.key(seed), 9)
    frames = gaussian(splits[0], (2, N_CTX * FRAMES, CELLS, C_ENC), 1.0, 6.0, ((0, 2), (1, 4)))
    w_conv = gaussian(splits[1], (3, C_ENC, C_ENC), (3 * C_ENC) ** -0.5, 0.15625)
    w_lat = gaussian(splits[2], (C_ENC, LATC), C_ENC ** -0.5, 0.25)
    dest_keys = jax.random.split(jax.random.fold_in(splits[3], 1), 2 * TOKENS // ROWS)
    dest_turns = jax.random.permutation(jax.random.fold_in(splits[3], 3), 2 * TOKENS // ROWS)
    dest = jax.vmap(lambda own, number: assign_block(jax.random.fold_in(splits[3], 2), own, number, ROWS, N_CTX, 1, CAP, 2))(dest_keys, dest_turns).reshape((2, TOKENS, 1))
    pick = set_ends(jax.random.randint(splits[4], (2, TOKENS), 0, 7), jax.random.fold_in(splits[4], 1), 0, 6).astype(jnp.int32)
    w_embed = gaussian(splits[5], (LATENT, D), LATENT ** -0.5, 0.75)
    gain = jnp.clip(1.0 + 0.15 * jax.random.normal(splits[6], (D,), jnp.float32), 0.25, 1.75)
    w_qkv = gaussian(splits[7], (D, 3, HEADS * HEAD), D ** -0.5, 0.078125, ((2, 4),))
    return {"frames": frames, "w_conv": w_conv, "w_lat": w_lat, "dest": dest, "pick": pick, "w_embed": w_embed, "gain": gain, "w_qkv": w_qkv}


def encode(frame_block, w_conv, w_lat):
    frame_count = frame_block.shape[0]
    cells_here = frame_block.shape[1]
    channels = frame_block.shape[2]
    empty_frame = jnp.zeros_like(frame_block[:1])
    back_one = jnp.concatenate([empty_frame, frame_block[:-1]], axis=0)
    back_two = jnp.concatenate([empty_frame, empty_frame, frame_block[:-2]], axis=0)
    hidden = jnp.dot(frame_block.reshape(-1, channels), w_conv[0], preferred_element_type=jnp.float32)
    hidden = hidden + jnp.dot(back_one.reshape(-1, channels), w_conv[1], preferred_element_type=jnp.float32)
    hidden = hidden + jnp.dot(back_two.reshape(-1, channels), w_conv[2], preferred_element_type=jnp.float32)
    active = jax.nn.silu(hidden).astype(jnp.bfloat16)
    latent = jnp.dot(active, w_lat, preferred_element_type=jnp.float32).astype(jnp.bfloat16)
    return latent.reshape(frame_count, cells_here // 4, 4 * w_lat.shape[1])

def head_norm(values):
    return values * lax.rsqrt(lax.optimization_barrier(jnp.mean(values * values, axis=-1, keepdims=True)) + 1e-06)

def reference(frames, w_conv, w_lat, dest, pick, w_embed, gain, w_qkv):
    footage = frames.reshape(2, N_CTX, FRAMES, CELLS, C_ENC)
    results = []
    for section_slot in range(2):
        source = 1 - section_slot
        patch_rows = jnp.stack([encode(footage[source, shard], w_conv, w_lat).reshape(ROWS, LATENT) for shard in range(N_CTX)])
        targets = dest[source, :, 0].reshape(N_CTX, ROWS).astype(jnp.int32)
        choose = pick[source].reshape(N_CTX, ROWS).astype(jnp.int32)
        tier = (choose >= 4).astype(jnp.int32) + (choose >= 6).astype(jnp.int32)
        labels = targets // GROUP + NGROUP * tier + 1
        onehot = (targets[:, :, None] == jnp.arange(N_CTX, dtype=jnp.int32)[None, None, :]).astype(jnp.int32)
        before = jnp.cumsum(onehot, axis=1, dtype=jnp.int32) - onehot
        within = lax.optimization_barrier(jnp.sum(before * onehot, axis=2, dtype=jnp.int32))
        position = targets * (N_CTX * CAP) + jnp.arange(N_CTX, dtype=jnp.int32)[:, None] * CAP + within
        tokens = patch_rows.reshape(-1, LATENT)
        flat_labels = labels.reshape(-1)
        embedded = jnp.dot(tokens, w_embed, preferred_element_type=jnp.float32)
        normed = (embedded * lax.rsqrt(lax.optimization_barrier(jnp.mean(embedded * embedded, axis=-1, keepdims=True)) + 1e-06) * gain).astype(jnp.bfloat16)
        projected = jnp.dot(normed, w_qkv.reshape(D, -1), preferred_element_type=jnp.float32)
        projected = projected.reshape(-1, 3, HEADS, HEAD)
        queries = head_norm(projected[:, 0]).astype(jnp.bfloat16)
        keys_all = head_norm(projected[:, 1]).astype(jnp.bfloat16)
        values_all = projected[:, 2].astype(jnp.bfloat16)
        allowed = flat_labels[:, None] == flat_labels[None, :]
        factor = 1.0 / HEAD ** 0.5

        def one_head(operands):
            query_head, key_head, value_head = operands
            scores = jnp.dot(query_head, key_head.T, preferred_element_type=jnp.float32) * factor
            expo = jnp.where(allowed, jnp.exp(scores), 0.0)
            total = lax.optimization_barrier(jnp.sum(expo, axis=-1))
            summed = jnp.dot(expo.astype(jnp.bfloat16), value_head, preferred_element_type=jnp.float32)
            return summed / total[:, None]
        heads_out = lax.map(one_head, (queries.transpose(1, 0, 2), keys_all.transpose(1, 0, 2), values_all.transpose(1, 0, 2)))
        attended = heads_out.transpose(1, 0, 2).reshape(-1, HEADS * HEAD).astype(jnp.bfloat16)
        canvas = jnp.zeros((N_CTX * N_CTX * CAP, HEADS * HEAD), jnp.bfloat16)
        results.append(canvas.at[position.reshape(-1)].set(attended))
    return jnp.stack(results)
```

```python
import functools

import jax
import jax.numpy as jnp
from jax import lax
from jax.experimental import pallas as pl
from jax.experimental.pallas import tpu as pltpu
from jax.sharding import PartitionSpec as P

HEAD = 128
GROUP = 4
LANES = 128
META = 16
EPS = 1e-06
MESH = pl.DeviceIdType.MESH
F32 = jnp.float32
BF16 = jnp.bfloat16
ANY = pl.BlockSpec(memory_space=pl.ANY)
VMEM = pl.BlockSpec(memory_space=pltpu.VMEM)


def dot(a, b):
    return jnp.dot(a, b, preferred_element_type=F32)


def dot_nt(a, b):
    return lax.dot_general(a, b, (((1,), (1,)), ((), ())), preferred_element_type=F32)


def iota(shape, dim):
    return lax.broadcasted_iota(jnp.int32, shape, dim)


def encode_kernel(
    shards, frame_count, pieces,
    frames_hbm, conv_hbm, lat_ref, dest_ref, pick_ref, embed_hbm, gain_ref, qkv_hbm,
    rows_out, weff_out,
    frames, conv, embed, qkv, scaled, hidden, outgoing, mine,
    in_sem, qkv_sem, row_send, row_recv, half_send, half_recv, keep_sem,
):
    section = lax.axis_index("section")
    ctx = lax.axis_index("ctx")
    other = 1 - section
    depth = embed.shape[1]
    latent = embed.shape[0]
    half = qkv.shape[2]
    step = depth // pieces
    row_count = outgoing.shape[0] - META

    loads = [
        pltpu.make_async_copy(frames_hbm, frames, in_sem.at[0]),
        pltpu.make_async_copy(conv_hbm, conv, in_sem.at[1]),
        pltpu.make_async_copy(embed_hbm, embed, in_sem.at[2]),
    ]
    for load in loads:
        load.start()
    columns = pl.ds(pl.multiple_of(section * half, LANES), half)
    streams = []
    for j in range(3):
        for p in range(pieces):
            part = pl.ds(p * step, step)
            stream = pltpu.make_async_copy(
                qkv_hbm.at[j, part, columns], qkv.at[j, part, :], qkv_sem.at[j * pieces + p]
            )
            stream.start()
            streams.append(stream)

    barrier = pltpu.get_barrier_semaphore()
    for d in range(shards):
        pl.semaphore_signal(
            barrier, inc=1,
            device_id={"section": other, "ctx": lax.rem(ctx + d, shards)}, device_id_type=MESH,
        )

    first = section == 0
    dest = jnp.where(first, dest_ref[0], dest_ref[1])
    pick = jnp.where(first, pick_ref[0:1, :], pick_ref[1:2, :])
    tier = (pick >= 4).astype(jnp.int32) + (pick >= 6).astype(jnp.int32)
    label = dest // GROUP + shards // GROUP * tier + 1
    padded = -(-shards // 8) * 8
    onehot = (iota((padded, row_count), 0) == dest).astype(F32)
    earlier = (iota((row_count, row_count), 0) < iota((row_count, row_count), 1)).astype(F32)
    before = dot(onehot.astype(BF16), earlier.astype(BF16))
    within = jnp.sum(before * onehot, axis=0, keepdims=True)
    line = iota((META, row_count), 0)
    meta = jnp.where(line == 0, dest.astype(F32), 0.0)
    meta = jnp.where(line == 1, within, meta)
    meta = jnp.where(line == 2, label.astype(F32), meta)
    outgoing[row_count:, :] = meta.astype(BF16)

    loads[0].wait()
    loads[1].wait()
    cells = frames.shape[0]
    frame = cells // frame_count
    hidden[...] = dot(frames[...], conv[0])
    hidden[frame:, :] += dot(frames[: cells - frame, :], conv[1])
    hidden[2 * frame :, :] += dot(frames[: cells - 2 * frame, :], conv[2])
    value = hidden[...]
    active = (value * jax.nn.sigmoid(value)).astype(BF16)
    channels = lat_ref.shape[0]
    per = latent // channels
    narrow = dot_nt(active, lat_ref[...]).astype(BF16)
    lane = iota((channels, LANES), 1)
    spread = ((lane % channels == iota((channels, LANES), 0)) & (lane < latent)).astype(F32)
    wide = dot(narrow, spread.astype(BF16))
    wide = jnp.where(
        iota((cells, LANES), 1) // channels == iota((cells, LANES), 0) % per, wide, 0.0
    ).astype(BF16)
    gather = (iota((row_count, cells), 1) // per == iota((row_count, cells), 0)).astype(F32)
    patches = dot(gather.astype(BF16), wide)
    loads[2].wait()
    narrow_patches = patches[:, :latent].astype(BF16)
    square = jnp.zeros((row_count, LANES), F32)
    tile = 512
    for k in range(depth // tile):
        x = dot(narrow_patches, embed[:, k * tile : (k + 1) * tile])
        x = x * x
        for i in range(tile // LANES):
            square = square + x[:, i * LANES : (i + 1) * LANES]
    scale = lax.rsqrt(jnp.sum(square, axis=1, keepdims=True) / depth + EPS)
    high = scale.astype(BF16).astype(F32)
    middle = (scale - high).astype(BF16).astype(F32)
    low = scale - high - middle
    lane = iota((row_count, LANES), 1)
    message = jnp.where(lane == latent, high, patches)
    message = jnp.where(lane == latent + 1, middle, message)
    message = jnp.where(lane == latent + 2, low, message)
    outgoing[:row_count, :] = message.astype(BF16)

    pl.semaphore_wait(barrier, shards)
    sends = []
    for d in range(shards):
        send = pltpu.make_async_remote_copy(
            src_ref=outgoing, dst_ref=rows_out.at[ctx],
            send_sem=row_send.at[d], recv_sem=row_recv.at[d],
            device_id={"section": other, "ctx": lax.rem(ctx + d, shards)}, device_id_type=MESH,
        )
        send.start()
        sends.append(send)

    for k in range(depth // tile):
        part = slice(k * tile, (k + 1) * tile)
        full = embed[:, part].astype(F32) * gain_ref[:, part]
        top = full.astype(BF16)
        scaled[:latent, part] = top
        scaled[latent:, part] = (full - top.astype(F32)).astype(BF16)

    keeps = []
    for j in range(3):
        total = jnp.zeros((2 * latent, half), F32)
        for p in range(pieces):
            streams[j * pieces + p].wait()
            part = slice(p * step, (p + 1) * step)
            total = total + dot(scaled[:, part], qkv[j, part, :])
        mine[j] = (total[:latent] + total[latent:]).astype(BF16)
        send = pltpu.make_async_remote_copy(
            src_ref=mine.at[j], dst_ref=weff_out.at[section, j],
            send_sem=half_send.at[j], recv_sem=half_recv.at[j],
            device_id={"section": other}, device_id_type=MESH,
        )
        send.start()
        sends.append(send)
        keep = pltpu.make_async_copy(mine.at[j], weff_out.at[section, j], keep_sem.at[j])
        keep.start()
        keeps.append(keep)
    for keep in keeps:
        keep.wait()
    for send in sends:
        send.wait()


def attend_kernel(shards, capacity, rows_ref, weff_ref, out_ref, picked_ref, row_ref, mask_ref):
    ctx = lax.axis_index("ctx")
    row_count = rows_ref.shape[1] - META
    latent = weff_ref.shape[2]
    half = weff_ref.shape[3]
    slots = out_ref.shape[0]
    total_rows = shards * row_count

    @pl.when(pl.program_id(0) == 0)
    def _():
        labels, spots = [], []
        for source in range(shards):
            meta = rows_ref[source, row_count:, :].astype(F32)
            labels.append(meta[2:3, :])
            home = meta[1:2, :] + (source * capacity)
            spots.append(jnp.where(meta[0:1, :] == ctx.astype(F32), home, -1.0))
            row_ref[source * row_count : (source + 1) * row_count, :] = rows_ref[source, :row_count, :]
        label = jnp.concatenate(labels, axis=1)
        spot = jnp.concatenate(spots, axis=1).astype(jnp.int32)
        taken = spot == iota((slots, total_rows), 0)
        picked_ref[...] = dot(taken.astype(F32).astype(BF16), row_ref[...]).astype(BF16)
        own = jnp.sum(jnp.where(taken, label, 0.0), axis=1, keepdims=True)
        mask_ref[...] = (label == own).astype(F32)

    def scale_of(block):
        return (
            block[:, latent : latent + 1].astype(F32)
            + block[:, latent + 1 : latent + 2].astype(F32)
            + block[:, latent + 2 : latent + 3].astype(F32)
        )

    def head_norm(x):
        return x * lax.rsqrt(jnp.mean(x * x, axis=-1, keepdims=True) + EPS)

    picked = picked_ref[...]
    everything = row_ref[...]
    picked_scale = scale_of(picked)
    row_scale = scale_of(everything)
    q = dot(picked[:, :latent], weff_ref[0, 0])
    k = dot(everything[:, :latent], weff_ref[0, 1])
    v = dot(everything[:, :latent], weff_ref[0, 2])
    allowed = mask_ref[...] > 0.5
    factor = 1.0 / HEAD**0.5
    for h in range(half // HEAD):
        part = slice(h * HEAD, (h + 1) * HEAD)
        queries = head_norm(q[:, part] * picked_scale).astype(BF16)
        keys = head_norm(k[:, part] * row_scale).astype(BF16)
        values = (v[:, part] * row_scale).astype(BF16)
        scores = dot_nt(queries, keys) * factor
        expo = jnp.where(allowed, jnp.exp(scores), 0.0)
        den = jnp.sum(expo, axis=1, keepdims=True)
        summed = dot(expo.astype(BF16), values)
        out_ref[:, part] = (summed / jnp.where(den > 0.0, den, 1.0)).astype(BF16)


def on_device(shards, sections, frames, w_conv, w_lat, dest, pick, w_embed, gain, w_qkv):
    _, frame_count, frame, channels = frames.shape
    latent, depth = w_embed.shape
    cells = frame_count * frame
    row_count = dest.shape[1]
    columns = w_qkv.shape[2]
    half = columns // sections
    pieces = 4
    capacity = max(2, 3 * row_count // (2 * shards))
    slots = shards * capacity
    rows, weff = pl.pallas_call(
        functools.partial(encode_kernel, shards, frame_count, pieces),
        out_shape=(
            jax.ShapeDtypeStruct((shards, row_count + META, LANES), BF16),
            jax.ShapeDtypeStruct((sections, 3, latent, half), BF16),
        ),
        in_specs=[ANY, ANY, VMEM, VMEM, VMEM, ANY, VMEM, ANY],
        out_specs=(ANY, ANY),
        scratch_shapes=[
            pltpu.VMEM((cells, channels), BF16),
            pltpu.VMEM(w_conv.shape, BF16),
            pltpu.VMEM((latent, depth), BF16),
            pltpu.VMEM((3, depth, half), BF16),
            pltpu.VMEM((2 * latent, depth), BF16),
            pltpu.VMEM((cells, channels), F32),
            pltpu.VMEM((row_count + META, LANES), BF16),
            pltpu.VMEM((3, latent, half), BF16),
            pltpu.SemaphoreType.DMA((3,)),
            pltpu.SemaphoreType.DMA((3 * pieces,)),
            pltpu.SemaphoreType.DMA((shards,)),
            pltpu.SemaphoreType.DMA((shards,)),
            pltpu.SemaphoreType.DMA((3,)),
            pltpu.SemaphoreType.DMA((3,)),
            pltpu.SemaphoreType.DMA((3,)),
        ],
        compiler_params=pltpu.CompilerParams(
            collective_id=0, has_side_effects=True, vmem_limit_bytes=48 << 20
        ),
    )(
        frames.reshape(cells, channels),
        w_conv,
        w_lat.T,
        dest.transpose(0, 2, 1),
        pick,
        w_embed,
        gain.reshape(1, depth),
        w_qkv.transpose(1, 0, 2),
    )
    out = pl.pallas_call(
        functools.partial(attend_kernel, shards, capacity),
        grid=(sections,),
        out_shape=jax.ShapeDtypeStruct((slots, columns), BF16),
        in_specs=[
            pl.BlockSpec((shards, row_count + META, LANES), lambda i: (0, 0, 0)),
            pl.BlockSpec((1, 3, latent, half), lambda i: (i, 0, 0, 0)),
        ],
        out_specs=pl.BlockSpec((slots, half), lambda i: (0, i)),
        scratch_shapes=[
            pltpu.VMEM((slots, LANES), BF16),
            pltpu.VMEM((shards * row_count, LANES), BF16),
            pltpu.VMEM((slots, shards * row_count), F32),
        ],
        compiler_params=pltpu.CompilerParams(vmem_limit_bytes=48 << 20),
    )(rows, weff)
    return out.reshape(1, slots, columns)


def solution(mesh):
    in_specs = (
        P("section", "ctx", None, None),
        P(),
        P(),
        P(None, "ctx", None),
        P(None, "ctx"),
        P(),
        P(),
        P(None, None, "mp"),
    )
    return jax.shard_map(
        functools.partial(on_device, mesh.shape["ctx"], mesh.shape["section"]),
        mesh=mesh,
        in_specs=in_specs,
        out_specs=P("section", "ctx", "mp"),
        check_vma=False,
    )
```

```python
import functools
import math

import jax
import jax.numpy as jnp
from jax import lax
from jax.experimental import pallas as pl
from jax.experimental.pallas import tpu as pltpu
from jax.sharding import PartitionSpec as P

HEAD = 128
GROUP = 4
LANES = 128
META = 16
EPS = 1e-06
BARRED = 16384.0
LOG2E = math.log2(math.e)
SPLIT = True
MESH = pl.DeviceIdType.MESH
F32 = jnp.float32
BF16 = jnp.bfloat16
HBM = pl.BlockSpec(memory_space=pltpu.HBM)


def dot(a, b):
    return jnp.dot(a, b, preferred_element_type=F32)


def dot_nt(a, b):
    return lax.dot_general(a, b, (((1,), (1,)), ((), ())), preferred_element_type=F32)


def iota(shape, dim):
    return lax.broadcasted_iota(jnp.int32, shape, dim)


def layer_kernel(
    shards, frame_count, pieces, capacity, split,
    frames_hbm, conv_hbm, lat_hbm, dest_hbm, pick_hbm, embed_hbm, gain_hbm, qkv_hbm,
    out_hbm,
    frames, conv, lat_ref, dest_ref, pick_ref, embed, gain_ref, qkv, scaled, hidden, outgoing, arrived, mine, theirs,
    scales, floors, tags, keys_ref, values_ref, result,
    in_sem, qkv_sem, row_send, row_recv, half_send, half_recv, out_sem,
):
    section = lax.axis_index("section")
    ctx = lax.axis_index("ctx")
    other = 1 - section
    depth = embed.shape[1]
    latent = embed.shape[0]
    half = qkv.shape[2]
    step = depth // pieces
    row_count = outgoing.shape[0] - META

    loads = [
        pltpu.make_async_copy(source, target, in_sem.at[i])
        for i, (source, target) in enumerate((
            (embed_hbm, embed), (gain_hbm, gain_ref), (dest_hbm, dest_ref), (pick_hbm, pick_ref),
            (frames_hbm, frames), (conv_hbm, conv), (lat_hbm, lat_ref),
        ))
    ]
    for load in loads:
        load.start()
    columns = pl.ds(pl.multiple_of(section * half, LANES), half)
    streams = []
    for j in range(3):
        for p in range(pieces):
            part = pl.ds(p * step, step)
            stream = pltpu.make_async_copy(
                qkv_hbm.at[j, part, columns], qkv.at[j, part, :], qkv_sem.at[j * pieces + p]
            )
            stream.start()
            streams.append(stream)

    barrier = pltpu.get_barrier_semaphore()
    for d in range(shards):
        pl.semaphore_signal(
            barrier, inc=1,
            device_id={"section": other, "ctx": lax.rem(ctx + d, shards)}, device_id_type=MESH,
        )

    loads[0].wait()
    loads[1].wait()
    tile = 512
    for k in range(depth // tile):
        part = slice(k * tile, (k + 1) * tile)
        full = embed[:, part].astype(F32) * gain_ref[:, part]
        top = full.astype(BF16)
        scaled[:latent, part] = top
        if split:
            scaled[latent:, part] = (full - top.astype(F32)).astype(BF16)

    loads[2].wait()
    loads[3].wait()
    first = section == 0
    dest = jnp.where(first, dest_ref[0], dest_ref[1])
    pick = jnp.where(first, pick_ref[0:1, :], pick_ref[1:2, :])
    tier = (pick >= 4).astype(jnp.int32) + (pick >= 6).astype(jnp.int32)
    label = dest // GROUP + shards // GROUP * tier + 1
    padded = -(-shards // 8) * 8
    onehot = (iota((padded, row_count), 0) == dest).astype(F32)
    earlier = (iota((row_count, row_count), 0) < iota((row_count, row_count), 1)).astype(F32)
    before = dot(onehot.astype(BF16), earlier.astype(BF16))
    within = jnp.sum(before * onehot, axis=0, keepdims=True)
    line = iota((META, row_count), 0)
    meta = jnp.where(line == 0, dest.astype(F32), 0.0)
    meta = jnp.where(line == 1, within, meta)
    meta = jnp.where(line == 2, label.astype(F32), meta)
    outgoing[row_count:, :] = meta.astype(BF16)

    loads[4].wait()
    loads[5].wait()
    cells = frames.shape[0]
    frame = cells // frame_count
    hidden[...] = dot(frames[...], conv[0])
    hidden[frame:, :] += dot(frames[: cells - frame, :], conv[1])
    hidden[2 * frame :, :] += dot(frames[: cells - 2 * frame, :], conv[2])
    value = hidden[...]
    active = (value * jax.nn.sigmoid(value)).astype(BF16)
    loads[6].wait()
    channels = lat_ref.shape[0]
    per = latent // channels
    narrow = dot_nt(active, lat_ref[...]).astype(BF16)
    lane = iota((channels, LANES), 1)
    spread = ((lane % channels == iota((channels, LANES), 0)) & (lane < latent)).astype(F32)
    wide = dot(narrow, spread.astype(BF16))
    wide = jnp.where(
        iota((cells, LANES), 1) // channels == iota((cells, LANES), 0) % per, wide, 0.0
    ).astype(BF16)
    gather = (iota((row_count, cells), 1) // per == iota((row_count, cells), 0)).astype(F32)
    patches = dot(gather.astype(BF16), wide)
    narrow_patches = patches[:, :latent].astype(BF16)
    square = jnp.zeros((row_count, LANES), F32)
    for k in range(depth // tile):
        x = dot(narrow_patches, embed[:, k * tile : (k + 1) * tile])
        x = x * x
        for i in range(tile // LANES):
            square = square + x[:, i * LANES : (i + 1) * LANES]
    scale = lax.rsqrt(jnp.sum(square, axis=1, keepdims=True) / depth + EPS)
    high = scale.astype(BF16).astype(F32)
    middle = (scale - high).astype(BF16).astype(F32)
    low = scale - high - middle
    lane = iota((row_count, LANES), 1)
    line = iota((row_count, LANES), 0)
    placed = jnp.where(line == latent + 3, label, 0).astype(F32).astype(BF16)
    message = patches + dot_nt((line == lane).astype(F32).astype(BF16), placed)
    message = jnp.where(lane == latent, high, message)
    message = jnp.where(lane == latent + 1, middle, message)
    message = jnp.where(lane == latent + 2, low, message)
    outgoing[:row_count, :] = message.astype(BF16)

    pl.semaphore_wait(barrier, shards)
    sends = []
    for d in range(shards):
        send = pltpu.make_async_remote_copy(
            src_ref=outgoing, dst_ref=arrived.at[ctx],
            send_sem=row_send.at[d], recv_sem=row_recv.at[d],
            device_id={"section": other, "ctx": lax.rem(ctx + d, shards)}, device_id_type=MESH,
        )
        send.start()
        sends.append(send)

    halves = []
    for j in range(3):
        total = jnp.zeros((scaled.shape[0], half), F32)
        for p in range(pieces):
            streams[j * pieces + p].wait()
            part = slice(p * step, (p + 1) * step)
            total = total + dot(scaled[:, part], qkv[j, part, :])
        if split:
            total = total[:latent] + total[latent:]
        mine[j] = total.astype(BF16)
        send = pltpu.make_async_remote_copy(
            src_ref=mine.at[j], dst_ref=theirs.at[j],
            send_sem=half_send.at[j], recv_sem=half_recv.at[j],
            device_id={"section": other}, device_id_type=MESH,
        )
        send.start()
        halves.append(send)

    for send in sends:
        send.wait()
    slots = shards * capacity
    mine_here = ctx.astype(F32)
    spots = []
    lane = iota((row_count, LANES), 1)

    def constants(block):
        scale = (
            block[:, latent : latent + 1].astype(F32)
            + block[:, latent + 1 : latent + 2].astype(F32)
            + block[:, latent + 2 : latent + 3].astype(F32)
        )
        return scale, block[:, latent + 3 : latent + 4].astype(F32).astype(jnp.int32)

    for source in range(shards):
        meta = arrived[source, row_count:, :].astype(F32)
        spots.append(jnp.where(meta[0:1, :] == mine_here, meta[1:2, :] + source * capacity, -1.0))
        scale, tag = constants(arrived[source, :row_count, :])
        part = slice(source * row_count, (source + 1) * row_count)
        scales[part, :] = jnp.broadcast_to(scale, (row_count, LANES))
        floors[part, :] = jnp.broadcast_to(HEAD * EPS / (scale * scale), (row_count, LANES))
        tags[part, :] = (lane == tag).astype(F32).astype(BF16)
    picked = jnp.zeros((slots, LANES), F32)
    for source in range(shards):
        taken = spots[source].astype(jnp.int32) == iota((slots, row_count), 0)
        picked = picked + dot(taken.astype(F32).astype(BF16), arrived[source, :row_count, :])
    picked = picked.astype(BF16)
    picked_scale, picked_tag = constants(picked)
    picked_scale = jnp.where(picked_tag > 0, picked_scale, 1.0)
    picked_floor = HEAD * EPS / (picked_scale * picked_scale)
    barred = jnp.where(iota((slots, LANES), 1) == picked_tag, 0.0, -BARRED).astype(BF16)
    barred = jnp.where(picked_tag > 0, barred.astype(F32), -BARRED).astype(BF16)
    ones = jnp.ones((shards * row_count, HEAD), BF16)
    gain_q = HEAD**0.5 * LOG2E

    writes = []
    for side, weff in ((0, mine), (1, theirs)):
        if side == 1:
            for send in halves:
                send.wait()
        width = min(half, 2 * HEAD)
        for group in range(half // width):
            part = slice(group * width, (group + 1) * width)
            for source in range(shards):
                block = arrived[source, :row_count, :latent]
                k = dot(block, weff[1, :, part])
                v = dot(block, weff[2, :, part])
                rows = slice(source * row_count, (source + 1) * row_count)
                for h in range(width // HEAD):
                    kh = k[:, h * HEAD : (h + 1) * HEAD]
                    power = jnp.sum(kh * kh, axis=1, keepdims=True) + floors[rows, :]
                    keys_ref[group * (width // HEAD) + h, rows, :] = (kh * lax.rsqrt(power)).astype(BF16)
                    vh = v[:, h * HEAD : (h + 1) * HEAD]
                    values_ref[group * (width // HEAD) + h, rows, :] = (vh * scales[rows, :]).astype(BF16)
            q = dot(picked[:, :latent], weff[0, :, part])
            for h in range(width // HEAD):
                head = group * (width // HEAD) + h
                qh = q[:, h * HEAD : (h + 1) * HEAD]
                power = jnp.sum(qh * qh, axis=1, keepdims=True) + picked_floor
                queries = (qh * (lax.rsqrt(power) * gain_q)).astype(BF16)
                scores = dot_nt(
                    jnp.concatenate([queries, barred], axis=1),
                    jnp.concatenate([keys_ref[head], tags[...]], axis=1),
                )
                weights = jnp.exp2(scores).astype(BF16)
                both = dot(weights, jnp.concatenate([values_ref[head], ones], axis=1))
                den = both[:, HEAD:]
                result[side, :, head * HEAD : (head + 1) * HEAD] = (
                    both[:, :HEAD] / jnp.where(den > 0.0, den, 1.0)
                ).astype(BF16)
        where = pl.ds(pl.multiple_of((section if side == 0 else other) * half, LANES), half)
        write = pltpu.make_async_copy(result.at[side], out_hbm.at[:, where], out_sem.at[side])
        write.start()
        writes.append(write)
    for write in writes:
        write.wait()


def on_device(shards, sections, frames, w_conv, w_lat, dest, pick, w_embed, gain, w_qkv):
    _, frame_count, frame, channels = frames.shape
    latent, depth = w_embed.shape
    cells = frame_count * frame
    row_count = dest.shape[1]
    columns = w_qkv.shape[2]
    half = columns // sections
    pieces = 4
    split = SPLIT
    capacity = max(2, 3 * row_count // (2 * shards))
    slots = shards * capacity
    total_rows = shards * row_count
    out = pl.pallas_call(
        functools.partial(layer_kernel, shards, frame_count, pieces, capacity, split),
        out_shape=jax.ShapeDtypeStruct((slots, columns), BF16),
        in_specs=[HBM] * 8,
        out_specs=HBM,
        scratch_shapes=[
            pltpu.VMEM((cells, channels), BF16),
            pltpu.VMEM(w_conv.shape, BF16),
            pltpu.VMEM((w_lat.shape[1], channels), BF16),
            pltpu.VMEM((sections, 1, row_count), jnp.int32),
            pltpu.VMEM((sections, row_count), jnp.int32),
            pltpu.VMEM((latent, depth), BF16),
            pltpu.VMEM((1, depth), F32),
            pltpu.VMEM((3, depth, half), BF16),
            pltpu.VMEM((2 * latent if split else latent, depth), BF16),
            pltpu.VMEM((cells, channels), F32),
            pltpu.VMEM((row_count + META, LANES), BF16),
            pltpu.VMEM((shards, row_count + META, LANES), BF16),
            pltpu.VMEM((3, latent, half), BF16),
            pltpu.VMEM((3, latent, half), BF16),
            pltpu.VMEM((total_rows, LANES), F32),
            pltpu.VMEM((total_rows, LANES), F32),
            pltpu.VMEM((total_rows, LANES), BF16),
            pltpu.VMEM((half // HEAD, total_rows, HEAD), BF16),
            pltpu.VMEM((half // HEAD, total_rows, HEAD), BF16),
            pltpu.VMEM((sections, slots, half), BF16),
            pltpu.SemaphoreType.DMA((7,)),
            pltpu.SemaphoreType.DMA((3 * pieces,)),
            pltpu.SemaphoreType.DMA((shards,)),
            pltpu.SemaphoreType.DMA((shards,)),
            pltpu.SemaphoreType.DMA((3,)),
            pltpu.SemaphoreType.DMA((3,)),
            pltpu.SemaphoreType.DMA((2,)),
        ],
        compiler_params=pltpu.CompilerParams(
            collective_id=0, has_side_effects=True, vmem_limit_bytes=67043328
        ),
    )(
        frames.reshape(cells, channels),
        w_conv,
        w_lat.T,
        dest.transpose(0, 2, 1),
        pick,
        w_embed,
        gain.reshape(1, depth),
        w_qkv.transpose(1, 0, 2),
    )
    return out.reshape(1, slots, columns)


def solution(mesh):
    in_specs = (
        P("section", "ctx", None, None),
        P(),
        P(),
        P(None, "ctx", None),
        P(None, "ctx"),
        P(),
        P(),
        P(None, None, "mp"),
    )
    return jax.shard_map(
        functools.partial(on_device, mesh.shape["ctx"], mesh.shape["section"]),
        mesh=mesh,
        in_specs=in_specs,
        out_specs=P("section", "ctx", "mp"),
        check_vma=False,
    )
```

```python
import functools
import math

import jax
import jax.numpy as jnp
from jax import lax
from jax.experimental import pallas as pl
from jax.experimental.pallas import tpu as pltpu
from jax.sharding import PartitionSpec as P

HEAD = 128
GROUP = 4
LANES = 128
META = 16
EPS = 1e-06
BARRED = 16384.0
LOG2E = math.log2(math.e)
SPLIT = True
MESH = pl.DeviceIdType.MESH
F32 = jnp.float32
BF16 = jnp.bfloat16
HBM = pl.BlockSpec(memory_space=pltpu.HBM)


def dot(a, b):
    return jnp.dot(a, b, preferred_element_type=F32)


def dot_nt(a, b):
    return lax.dot_general(a, b, (((1,), (1,)), ((), ())), preferred_element_type=F32)


def iota(shape, dim):
    return lax.broadcasted_iota(jnp.int32, shape, dim)


def encode_kernel(
    shards, frame_count, pieces, split,
    frames_hbm, conv_hbm, lat_hbm, dest_hbm, pick_hbm, embed_hbm, gain_hbm, qkv_hbm,
    rows_out, weff_out,
    frames, conv, lat_ref, dest_ref, pick_ref, embed, gain_ref, qkv, scaled, hidden, outgoing, mine, total,
    in_sem, qkv_sem, row_send, row_recv, half_send, half_recv, keep_sem,
):
    section = lax.axis_index("section")
    ctx = lax.axis_index("ctx")
    other = 1 - section
    depth = embed.shape[1]
    latent = embed.shape[0]
    half = qkv.shape[2]
    step = depth // pieces
    row_count = outgoing.shape[0] - META

    loads = [
        pltpu.make_async_copy(source, target, in_sem.at[i])
        for i, (source, target) in enumerate((
            (embed_hbm, embed), (gain_hbm, gain_ref), (dest_hbm, dest_ref), (pick_hbm, pick_ref),
            (frames_hbm, frames), (conv_hbm, conv), (lat_hbm, lat_ref),
        ))
    ]
    for load in loads:
        load.start()
    columns = pl.ds(pl.multiple_of(section * half, LANES), half)

    def stream(j, p):
        part = pl.ds(pl.multiple_of(p * step, step), step)
        return pltpu.make_async_copy(
            qkv_hbm.at[j, part, columns], qkv.at[j, part, :], qkv_sem.at[j * pieces + p]
        )

    for j in range(3):
        for p in range(pieces):
            stream(j, p).start()

    barrier = pltpu.get_barrier_semaphore()
    for d in range(shards):
        pl.semaphore_signal(
            barrier, inc=1,
            device_id={"section": other, "ctx": lax.rem(ctx + d, shards)}, device_id_type=MESH,
        )

    loads[0].wait()
    loads[1].wait()
    tile = 512

    def scale_part(k, carry):
        part = pl.ds(pl.multiple_of(k * tile, tile), tile)
        full = embed[:, part].astype(F32) * gain_ref[:, part]
        top = full.astype(BF16)
        scaled[:latent, part] = top
        if split:
            scaled[latent:, part] = (full - top.astype(F32)).astype(BF16)
        return carry

    lax.fori_loop(0, depth // tile, scale_part, 0)

    loads[2].wait()
    loads[3].wait()
    first = section == 0
    dest = jnp.where(first, dest_ref[0], dest_ref[1])
    pick = jnp.where(first, pick_ref[0:1, :], pick_ref[1:2, :])
    tier = (pick >= 4).astype(jnp.int32) + (pick >= 6).astype(jnp.int32)
    label = dest // GROUP + shards // GROUP * tier + 1
    padded = -(-shards // 8) * 8
    onehot = (iota((padded, row_count), 0) == dest).astype(F32)
    earlier = (iota((row_count, row_count), 0) < iota((row_count, row_count), 1)).astype(F32)
    before = dot(onehot.astype(BF16), earlier.astype(BF16))
    within = jnp.sum(before * onehot, axis=0, keepdims=True)
    line = iota((META, row_count), 0)
    meta = jnp.where(line == 0, dest.astype(F32), 0.0)
    meta = jnp.where(line == 1, within, meta)
    meta = jnp.where(line == 2, label.astype(F32), meta)
    outgoing[row_count:, :] = meta.astype(BF16)

    loads[4].wait()
    loads[5].wait()
    cells = frames.shape[0]
    frame = cells // frame_count
    hidden[...] = dot(frames[...], conv[0])
    hidden[frame:, :] += dot(frames[: cells - frame, :], conv[1])
    hidden[2 * frame :, :] += dot(frames[: cells - 2 * frame, :], conv[2])
    value = hidden[...]
    active = (value * jax.nn.sigmoid(value)).astype(BF16)
    loads[6].wait()
    channels = lat_ref.shape[0]
    per = latent // channels
    narrow = dot_nt(active, lat_ref[...]).astype(BF16)
    lane = iota((channels, LANES), 1)
    spread = ((lane % channels == iota((channels, LANES), 0)) & (lane < latent)).astype(F32)
    wide = dot(narrow, spread.astype(BF16))
    wide = jnp.where(
        iota((cells, LANES), 1) // channels == iota((cells, LANES), 0) % per, wide, 0.0
    ).astype(BF16)
    gather = (iota((row_count, cells), 1) // per == iota((row_count, cells), 0)).astype(F32)
    patches = dot(gather.astype(BF16), wide)
    narrow_patches = patches[:, :latent].astype(BF16)

    def norm_part(k, square):
        x = dot(narrow_patches, embed[:, pl.ds(pl.multiple_of(k * tile, tile), tile)])
        x = x * x
        for i in range(tile // LANES):
            square = square + x[:, i * LANES : (i + 1) * LANES]
        return square

    square = lax.fori_loop(0, depth // tile, norm_part, jnp.zeros((row_count, LANES), F32))
    scale = lax.rsqrt(jnp.sum(square, axis=1, keepdims=True) / depth + EPS)
    high = scale.astype(BF16).astype(F32)
    middle = (scale - high).astype(BF16).astype(F32)
    low = scale - high - middle
    lane = iota((row_count, LANES), 1)
    line = iota((row_count, LANES), 0)
    placed = jnp.where(line == latent + 3, label, 0).astype(F32).astype(BF16)
    message = patches + dot_nt((line == lane).astype(F32).astype(BF16), placed)
    message = jnp.where(lane == latent, high, message)
    message = jnp.where(lane == latent + 1, middle, message)
    message = jnp.where(lane == latent + 2, low, message)
    outgoing[:row_count, :] = message.astype(BF16)

    pl.semaphore_wait(barrier, shards)
    sends = []
    for d in range(shards):
        send = pltpu.make_async_remote_copy(
            src_ref=outgoing, dst_ref=rows_out.at[ctx],
            send_sem=row_send.at[d], recv_sem=row_recv.at[d],
            device_id={"section": other, "ctx": lax.rem(ctx + d, shards)}, device_id_type=MESH,
        )
        send.start()
        sends.append(send)

    def swap(j):
        return pltpu.make_async_remote_copy(
            src_ref=mine.at[j], dst_ref=weff_out.at[section, j],
            send_sem=half_send.at[j], recv_sem=half_recv.at[j],
            device_id={"section": other}, device_id_type=MESH,
        )

    def keep(j):
        return pltpu.make_async_copy(mine.at[j], weff_out.at[section, j], keep_sem.at[j])

    def contract(j, carry):
        total[...] = jnp.zeros_like(total)

        def piece(p, inner):
            stream(j, p).wait()
            part = pl.ds(pl.multiple_of(p * step, step), step)
            total[...] += dot(scaled[:, part], qkv[j, part, :])
            return inner

        lax.fori_loop(0, pieces, piece, 0)
        full = total[...]
        if split:
            full = full[:latent] + full[latent:]
        mine[j] = full.astype(BF16)
        swap(j).start()
        keep(j).start()
        return carry

    lax.fori_loop(0, 3, contract, 0)
    for send in sends:
        send.wait()
    for j in range(3):
        keep(j).wait()
        swap(j).wait()


def attend_kernel(
    shards, capacity, rows_ref, weff_ref, out_ref,
    picked_ref, picked_floor, barred, rows, scales, floors, tags, keys_ref, values_ref,
):
    ctx = lax.axis_index("ctx").astype(F32)
    row_count = rows_ref.shape[1] - META
    latent, width = weff_ref.shape[2:]
    slots = out_ref.shape[0]

    @pl.when(pl.program_id(0) == 0)
    def _():
        def constants(block):
            scale = (
                block[:, latent : latent + 1].astype(F32)
                + block[:, latent + 1 : latent + 2].astype(F32)
                + block[:, latent + 2 : latent + 3].astype(F32)
            )
            return scale, block[:, latent + 3 : latent + 4].astype(F32).astype(jnp.int32)

        lane = iota((row_count, LANES), 1)
        picked = jnp.zeros((slots, LANES), F32)
        for source in range(shards):
            meta = rows_ref[source, row_count:, :].astype(F32)
            spot = jnp.where(meta[0:1, :] == ctx, meta[1:2, :] + source * capacity, -1.0)
            block = rows_ref[source, :row_count, :]
            taken = spot.astype(jnp.int32) == iota((slots, row_count), 0)
            picked = picked + dot(taken.astype(F32).astype(BF16), block)
            scale, tag = constants(block)
            part = slice(source * row_count, (source + 1) * row_count)
            rows[part, :] = block
            scales[part, :] = jnp.broadcast_to(scale, (row_count, LANES))
            floors[part, :] = jnp.broadcast_to(HEAD * EPS / (scale * scale), (row_count, LANES))
            tags[part, :] = (lane == tag).astype(F32).astype(BF16)
        picked = picked.astype(BF16)
        picked_ref[...] = picked
        scale, tag = constants(picked)
        scale = jnp.where(tag > 0, scale, 1.0)
        picked_floor[...] = jnp.broadcast_to(HEAD * EPS / (scale * scale), (slots, LANES))
        same = (iota((slots, LANES), 1) == tag) & (tag > 0)
        barred[...] = jnp.where(same, 0.0, -BARRED).astype(BF16)

    square_sum = (iota((width, width), 0) // HEAD == iota((width, width), 1) // HEAD)
    square_sum = square_sum.astype(F32).astype(BF16)
    ones = jnp.ones((rows.shape[0], HEAD), BF16)
    gain_q = HEAD**0.5 * LOG2E
    heads = [slice(h * HEAD, (h + 1) * HEAD) for h in range(width // HEAD)]

    for source in range(shards):
        part = slice(source * row_count, (source + 1) * row_count)
        block = rows[part, :latent]
        k = dot(block, weff_ref[0, 1])
        v = dot(block, weff_ref[0, 2])
        power = dot((k * k).astype(BF16), square_sum)
        for head in heads:
            keys_ref[part, head] = (k[:, head] * lax.rsqrt(power[:, head] + floors[part, :])).astype(BF16)
            values_ref[part, head] = (v[:, head] * scales[part, :]).astype(BF16)
    q = dot(picked_ref[:, :latent], weff_ref[0, 0])
    power = dot((q * q).astype(BF16), square_sum)
    for head in heads:
        scale = lax.rsqrt(power[:, head] + picked_floor[...]) * gain_q
        queries = (q[:, head] * scale).astype(BF16)
        scores = dot_nt(
            jnp.concatenate([queries, barred[...]], axis=1),
            jnp.concatenate([keys_ref[:, head], tags[...]], axis=1),
        )
        weights = jnp.exp2(scores).astype(BF16)
        both = dot(weights, jnp.concatenate([values_ref[:, head], ones], axis=1))
        den = both[:, HEAD:]
        out_ref[:, head] = (both[:, :HEAD] / jnp.where(den > 0.0, den, 1.0)).astype(BF16)


def on_device(shards, sections, frames, w_conv, w_lat, dest, pick, w_embed, gain, w_qkv):
    _, frame_count, frame, channels = frames.shape
    latent, depth = w_embed.shape
    cells = frame_count * frame
    row_count = dest.shape[1]
    columns = w_qkv.shape[2]
    half = columns // sections
    pieces = 4
    split = SPLIT
    capacity = max(2, 3 * row_count // (2 * shards))
    slots = shards * capacity
    total_rows = shards * row_count
    width = min(half, 2 * HEAD)
    groups = half // width
    rows, weff = pl.pallas_call(
        functools.partial(encode_kernel, shards, frame_count, pieces, split),
        out_shape=(
            jax.ShapeDtypeStruct((shards, row_count + META, LANES), BF16),
            jax.ShapeDtypeStruct((sections, 3, latent, half), BF16),
        ),
        in_specs=[HBM] * 8,
        out_specs=(HBM, HBM),
        scratch_shapes=[
            pltpu.VMEM((cells, channels), BF16),
            pltpu.VMEM(w_conv.shape, BF16),
            pltpu.VMEM((w_lat.shape[1], channels), BF16),
            pltpu.VMEM((sections, 1, row_count), jnp.int32),
            pltpu.VMEM((sections, row_count), jnp.int32),
            pltpu.VMEM((latent, depth), BF16),
            pltpu.VMEM((1, depth), F32),
            pltpu.VMEM((3, depth, half), BF16),
            pltpu.VMEM((2 * latent if split else latent, depth), BF16),
            pltpu.VMEM((cells, channels), F32),
            pltpu.VMEM((row_count + META, LANES), BF16),
            pltpu.VMEM((3, latent, half), BF16),
            pltpu.VMEM((2 * latent if split else latent, half), F32),
            pltpu.SemaphoreType.DMA((7,)),
            pltpu.SemaphoreType.DMA((3 * pieces,)),
            pltpu.SemaphoreType.DMA((shards,)),
            pltpu.SemaphoreType.DMA((shards,)),
            pltpu.SemaphoreType.DMA((3,)),
            pltpu.SemaphoreType.DMA((3,)),
            pltpu.SemaphoreType.DMA((3,)),
        ],
        compiler_params=pltpu.CompilerParams(
            collective_id=0, has_side_effects=True, vmem_limit_bytes=67043328
        ),
    )(
        frames.reshape(cells, channels),
        w_conv,
        w_lat.T,
        dest.transpose(0, 2, 1),
        pick,
        w_embed,
        gain.reshape(1, depth),
        w_qkv.transpose(1, 0, 2),
    )
    out = pl.pallas_call(
        functools.partial(attend_kernel, shards, capacity),
        grid=(sections * groups,),
        out_shape=jax.ShapeDtypeStruct((slots, columns), BF16),
        in_specs=[
            pl.BlockSpec((shards, row_count + META, LANES), lambda i: (0, 0, 0)),
            pl.BlockSpec((1, 3, latent, width), lambda i: (i // groups, 0, 0, i % groups)),
        ],
        out_specs=pl.BlockSpec((slots, width), lambda i: (0, i)),
        scratch_shapes=[
            pltpu.VMEM((slots, LANES), BF16),
            pltpu.VMEM((slots, LANES), F32),
            pltpu.VMEM((slots, LANES), BF16),
            pltpu.VMEM((total_rows, LANES), BF16),
            pltpu.VMEM((total_rows, LANES), F32),
            pltpu.VMEM((total_rows, LANES), F32),
            pltpu.VMEM((total_rows, LANES), BF16),
            pltpu.VMEM((total_rows, width), BF16),
            pltpu.VMEM((total_rows, width), BF16),
        ],
        compiler_params=pltpu.CompilerParams(vmem_limit_bytes=67043328),
    )(rows, weff)
    return out.reshape(1, slots, columns)


def solution(mesh):
    in_specs = (
        P("section", "ctx", None, None),
        P(),
        P(),
        P(None, "ctx", None),
        P(None, "ctx"),
        P(),
        P(),
        P(None, None, "mp"),
    )
    return jax.shard_map(
        functools.partial(on_device, mesh.shape["ctx"], mesh.shape["section"]),
        mesh=mesh,
        in_specs=in_specs,
        out_specs=P("section", "ctx", "mp"),
        check_vma=False,
    )
```

```python
import functools

import jax
import jax.numpy as jnp
from jax import lax
from jax.experimental import pallas as pl
from jax.experimental.pallas import tpu as pltpu
from jax.sharding import PartitionSpec as P

HEAD = 128
GROUP = 4
LANES = 128
META = 16
EPS = 1e-06
SPLIT = True
MESH = pl.DeviceIdType.MESH
F32 = jnp.float32
BF16 = jnp.bfloat16
HBM = pl.BlockSpec(memory_space=pltpu.HBM)


def dot(a, b):
    return jnp.dot(a, b, preferred_element_type=F32)


def dot_nt(a, b):
    return lax.dot_general(a, b, (((1,), (1,)), ((), ())), preferred_element_type=F32)


def iota(shape, dim):
    return lax.broadcasted_iota(jnp.int32, shape, dim)


def encode_kernel(
    shards, frame_count, pieces, split,
    frames_hbm, conv_hbm, lat_hbm, dest_hbm, pick_hbm, embed_hbm, gain_hbm, qkv_hbm,
    rows_out, weff_out,
    frames, conv, lat_ref, dest_ref, pick_ref, embed, gain_ref, qkv, scaled, hidden, outgoing, mine, total,
    in_sem, qkv_sem, row_send, row_recv, half_send, half_recv, keep_sem,
):
    section = lax.axis_index("section")
    ctx = lax.axis_index("ctx")
    other = 1 - section
    depth = embed.shape[1]
    latent = embed.shape[0]
    half = qkv.shape[2]
    step = depth // pieces
    row_count = outgoing.shape[0] - META

    loads = [
        pltpu.make_async_copy(source, target, in_sem.at[i])
        for i, (source, target) in enumerate((
            (embed_hbm, embed), (gain_hbm, gain_ref), (dest_hbm, dest_ref), (pick_hbm, pick_ref),
            (frames_hbm, frames), (conv_hbm, conv), (lat_hbm, lat_ref),
        ))
    ]
    for load in loads:
        load.start()
    columns = pl.ds(pl.multiple_of(section * half, LANES), half)

    def stream(j, p):
        part = pl.ds(pl.multiple_of(p * step, step), step)
        return pltpu.make_async_copy(
            qkv_hbm.at[j, part, columns], qkv.at[j, part, :], qkv_sem.at[j * pieces + p]
        )


    barrier = pltpu.get_barrier_semaphore()
    for d in range(shards):
        pl.semaphore_signal(
            barrier, inc=1,
            device_id={"section": other, "ctx": lax.rem(ctx + d, shards)}, device_id_type=MESH,
        )

    loads[0].wait()
    loads[1].wait()
    tile = 512

    def scale_part(k, carry):
        part = pl.ds(pl.multiple_of(k * tile, tile), tile)
        full = embed[:, part].astype(F32) * gain_ref[:, part]
        top = full.astype(BF16)
        scaled[:latent, part] = top
        if split:
            scaled[latent:, part] = (full - top.astype(F32)).astype(BF16)
        return carry

    lax.fori_loop(0, depth // tile, scale_part, 0)

    for load in loads[2:]:
        load.wait()
    for j in range(3):
        for p in range(pieces):
            stream(j, p).start()
    first = section == 0
    dest = jnp.where(first, dest_ref[0], dest_ref[1])
    pick = jnp.where(first, pick_ref[0:1, :], pick_ref[1:2, :])
    tier = (pick >= 4).astype(jnp.int32) + (pick >= 6).astype(jnp.int32)
    label = dest // GROUP + shards // GROUP * tier + 1
    padded = -(-shards // 8) * 8
    onehot = (iota((padded, row_count), 0) == dest).astype(F32)
    earlier = (iota((row_count, row_count), 0) < iota((row_count, row_count), 1)).astype(F32)
    before = dot(onehot.astype(BF16), earlier.astype(BF16))
    within = jnp.sum(before * onehot, axis=0, keepdims=True)
    line = iota((META, row_count), 0)
    meta = jnp.where(line == 0, dest.astype(F32), 0.0)
    meta = jnp.where(line == 1, within, meta)
    meta = jnp.where(line == 2, label.astype(F32), meta)
    outgoing[row_count:, :] = meta.astype(BF16)

    cells = frames.shape[0]
    frame = cells // frame_count
    hidden[...] = dot(frames[...], conv[0])
    hidden[frame:, :] += dot(frames[: cells - frame, :], conv[1])
    hidden[2 * frame :, :] += dot(frames[: cells - 2 * frame, :], conv[2])
    value = hidden[...]
    active = (value * jax.nn.sigmoid(value)).astype(BF16)
    channels = lat_ref.shape[0]
    per = latent // channels
    narrow = dot_nt(active, lat_ref[...]).astype(BF16)
    lane = iota((channels, LANES), 1)
    spread = ((lane % channels == iota((channels, LANES), 0)) & (lane < latent)).astype(F32)
    wide = dot(narrow, spread.astype(BF16))
    wide = jnp.where(
        iota((cells, LANES), 1) // channels == iota((cells, LANES), 0) % per, wide, 0.0
    ).astype(BF16)
    gather = (iota((row_count, cells), 1) // per == iota((row_count, cells), 0)).astype(F32)
    patches = dot(gather.astype(BF16), wide)
    narrow_patches = patches[:, :latent].astype(BF16)

    def norm_part(k, square):
        x = dot(narrow_patches, embed[:, pl.ds(pl.multiple_of(k * tile, tile), tile)])
        x = x * x
        for i in range(tile // LANES):
            square = square + x[:, i * LANES : (i + 1) * LANES]
        return square

    square = lax.fori_loop(0, depth // tile, norm_part, jnp.zeros((row_count, LANES), F32))
    scale = lax.rsqrt(jnp.sum(square, axis=1, keepdims=True) / depth + EPS)
    high = scale.astype(BF16).astype(F32)
    middle = (scale - high).astype(BF16).astype(F32)
    low = scale - high - middle
    lane = iota((row_count, LANES), 1)
    line = iota((row_count, LANES), 0)
    placed = jnp.where(line == latent + 3, label, 0).astype(F32).astype(BF16)
    message = patches + dot_nt((line == lane).astype(F32).astype(BF16), placed)
    message = jnp.where(lane == latent, high, message)
    message = jnp.where(lane == latent + 1, middle, message)
    message = jnp.where(lane == latent + 2, low, message)
    outgoing[:row_count, :] = message.astype(BF16)

    pl.semaphore_wait(barrier, shards)
    sends = []
    for d in range(shards):
        send = pltpu.make_async_remote_copy(
            src_ref=outgoing, dst_ref=rows_out.at[ctx],
            send_sem=row_send.at[d], recv_sem=row_recv.at[d],
            device_id={"section": other, "ctx": lax.rem(ctx + d, shards)}, device_id_type=MESH,
        )
        send.start()
        sends.append(send)

    def swap(j):
        return pltpu.make_async_remote_copy(
            src_ref=mine.at[j], dst_ref=weff_out.at[section, j],
            send_sem=half_send.at[j], recv_sem=half_recv.at[j],
            device_id={"section": other}, device_id_type=MESH,
        )

    def keep(j):
        return pltpu.make_async_copy(mine.at[j], weff_out.at[section, j], keep_sem.at[j])

    def contract(j, carry):
        total[...] = jnp.zeros_like(total)

        def piece(p, inner):
            stream(j, p).wait()
            part = pl.ds(pl.multiple_of(p * step, step), step)
            total[...] += dot(scaled[:, part], qkv[j, part, :])
            return inner

        lax.fori_loop(0, pieces, piece, 0)
        full = total[...]
        if split:
            full = full[:latent] + full[latent:]
        mine[j] = full.astype(BF16)
        swap(j).start()
        keep(j).start()
        return carry

    lax.fori_loop(0, 3, contract, 0)
    for send in sends:
        send.wait()
    for j in range(3):
        keep(j).wait()
        swap(j).wait()


def attend_kernel(shards, capacity, rows_ref, weff_ref, out_ref, picked_ref, row_ref, mask_ref):
    ctx = lax.axis_index("ctx")
    row_count = rows_ref.shape[1] - META
    latent = weff_ref.shape[2]
    half = weff_ref.shape[3]
    slots = out_ref.shape[0]
    total_rows = shards * row_count

    @pl.when(pl.program_id(0) == 0)
    def _():
        labels, spots = [], []
        for source in range(shards):
            meta = rows_ref[source, row_count:, :].astype(F32)
            labels.append(meta[2:3, :])
            home = meta[1:2, :] + (source * capacity)
            spots.append(jnp.where(meta[0:1, :] == ctx.astype(F32), home, -1.0))
            row_ref[source * row_count : (source + 1) * row_count, :] = rows_ref[source, :row_count, :]
        label = jnp.concatenate(labels, axis=1)
        spot = jnp.concatenate(spots, axis=1).astype(jnp.int32)
        taken = spot == iota((slots, total_rows), 0)
        picked_ref[...] = dot(taken.astype(F32).astype(BF16), row_ref[...]).astype(BF16)
        own = jnp.sum(jnp.where(taken, label, 0.0), axis=1, keepdims=True)
        mask_ref[...] = (label == own).astype(F32)

    def scale_of(block):
        return (
            block[:, latent : latent + 1].astype(F32)
            + block[:, latent + 1 : latent + 2].astype(F32)
            + block[:, latent + 2 : latent + 3].astype(F32)
        )

    def head_norm(x):
        return x * lax.rsqrt(jnp.mean(x * x, axis=-1, keepdims=True) + EPS)

    picked = picked_ref[...]
    everything = row_ref[...]
    picked_scale = scale_of(picked)
    row_scale = scale_of(everything)
    q = dot(picked[:, :latent], weff_ref[0, 0])
    k = dot(everything[:, :latent], weff_ref[0, 1])
    v = dot(everything[:, :latent], weff_ref[0, 2])
    allowed = mask_ref[...] > 0.5
    factor = 1.0 / HEAD**0.5
    for h in range(half // HEAD):
        part = slice(h * HEAD, (h + 1) * HEAD)
        queries = head_norm(q[:, part] * picked_scale).astype(BF16)
        keys = head_norm(k[:, part] * row_scale).astype(BF16)
        values = (v[:, part] * row_scale).astype(BF16)
        scores = dot_nt(queries, keys) * factor
        expo = jnp.where(allowed, jnp.exp(scores), 0.0)
        den = jnp.sum(expo, axis=1, keepdims=True)
        summed = dot(expo.astype(BF16), values)
        out_ref[:, part] = (summed / jnp.where(den > 0.0, den, 1.0)).astype(BF16)


def on_device(shards, sections, frames, w_conv, w_lat, dest, pick, w_embed, gain, w_qkv):
    _, frame_count, frame, channels = frames.shape
    latent, depth = w_embed.shape
    cells = frame_count * frame
    row_count = dest.shape[1]
    columns = w_qkv.shape[2]
    half = columns // sections
    pieces = 4
    split = SPLIT
    capacity = max(2, 3 * row_count // (2 * shards))
    slots = shards * capacity
    rows, weff = pl.pallas_call(
        functools.partial(encode_kernel, shards, frame_count, pieces, split),
        out_shape=(
            jax.ShapeDtypeStruct((shards, row_count + META, LANES), BF16),
            jax.ShapeDtypeStruct((sections, 3, latent, half), BF16),
        ),
        in_specs=[HBM] * 8,
        out_specs=(HBM, HBM),
        scratch_shapes=[
            pltpu.VMEM((cells, channels), BF16),
            pltpu.VMEM(w_conv.shape, BF16),
            pltpu.VMEM((w_lat.shape[1], channels), BF16),
            pltpu.VMEM((sections, 1, row_count), jnp.int32),
            pltpu.VMEM((sections, row_count), jnp.int32),
            pltpu.VMEM((latent, depth), BF16),
            pltpu.VMEM((1, depth), F32),
            pltpu.VMEM((3, depth, half), BF16),
            pltpu.VMEM((2 * latent if split else latent, depth), BF16),
            pltpu.VMEM((cells, channels), F32),
            pltpu.VMEM((row_count + META, LANES), BF16),
            pltpu.VMEM((3, latent, half), BF16),
            pltpu.VMEM((2 * latent if split else latent, half), F32),
            pltpu.SemaphoreType.DMA((7,)),
            pltpu.SemaphoreType.DMA((3 * pieces,)),
            pltpu.SemaphoreType.DMA((shards,)),
            pltpu.SemaphoreType.DMA((shards,)),
            pltpu.SemaphoreType.DMA((3,)),
            pltpu.SemaphoreType.DMA((3,)),
            pltpu.SemaphoreType.DMA((3,)),
        ],
        compiler_params=pltpu.CompilerParams(
            collective_id=0, has_side_effects=True, vmem_limit_bytes=67043328
        ),
    )(
        frames.reshape(cells, channels),
        w_conv,
        w_lat.T,
        dest.transpose(0, 2, 1),
        pick,
        w_embed,
        gain.reshape(1, depth),
        w_qkv.transpose(1, 0, 2),
    )
    out = pl.pallas_call(
        functools.partial(attend_kernel, shards, capacity),
        grid=(sections,),
        out_shape=jax.ShapeDtypeStruct((slots, columns), BF16),
        in_specs=[
            pl.BlockSpec((shards, row_count + META, LANES), lambda i: (0, 0, 0)),
            pl.BlockSpec((1, 3, latent, half), lambda i: (i, 0, 0, 0)),
        ],
        out_specs=pl.BlockSpec((slots, half), lambda i: (0, i)),
        scratch_shapes=[
            pltpu.VMEM((slots, LANES), BF16),
            pltpu.VMEM((shards * row_count, LANES), BF16),
            pltpu.VMEM((slots, shards * row_count), F32),
        ],
        compiler_params=pltpu.CompilerParams(vmem_limit_bytes=67043328),
    )(rows, weff)
    return out.reshape(1, slots, columns)


def solution(mesh):
    in_specs = (
        P("section", "ctx", None, None),
        P(),
        P(),
        P(None, "ctx", None),
        P(None, "ctx"),
        P(),
        P(),
        P(None, None, "mp"),
    )
    return jax.shard_map(
        functools.partial(on_device, mesh.shape["ctx"], mesh.shape["section"]),
        mesh=mesh,
        in_specs=in_specs,
        out_specs=P("section", "ctx", "mp"),
        check_vma=False,
    )
```

```python
import functools

import jax
import jax.numpy as jnp
from jax import lax
from jax.experimental import pallas as pl
from jax.experimental.pallas import tpu as pltpu
from jax.sharding import PartitionSpec as P

HEAD = 128
GROUP = 4
LANES = 128
META = 16
EPS = 1e-06
SPLIT = False
MESH = pl.DeviceIdType.MESH
F32 = jnp.float32
BF16 = jnp.bfloat16
HBM = pl.BlockSpec(memory_space=pltpu.HBM)


def dot(a, b):
    return jnp.dot(a, b, preferred_element_type=F32)


def dot_nt(a, b):
    return lax.dot_general(a, b, (((1,), (1,)), ((), ())), preferred_element_type=F32)


def iota(shape, dim):
    return lax.broadcasted_iota(jnp.int32, shape, dim)


def encode_kernel(
    shards, frame_count, pieces, split,
    frames_hbm, conv_hbm, lat_hbm, dest_hbm, pick_hbm, embed_hbm, gain_hbm, qkv_hbm,
    rows_out, weff_out,
    frames, conv, lat_ref, dest_ref, pick_ref, embed, gain_ref, qkv, scaled, hidden, outgoing, mine, total,
    in_sem, qkv_sem, row_send, row_recv, half_send, half_recv, keep_sem,
):
    section = lax.axis_index("section")
    ctx = lax.axis_index("ctx")
    other = 1 - section
    depth = embed.shape[1]
    latent = embed.shape[0]
    half = qkv.shape[2]
    step = depth // pieces
    row_count = outgoing.shape[0] - META

    loads = [
        pltpu.make_async_copy(source, target, in_sem.at[i])
        for i, (source, target) in enumerate((
            (embed_hbm, embed), (gain_hbm, gain_ref), (dest_hbm, dest_ref), (pick_hbm, pick_ref),
            (frames_hbm, frames), (conv_hbm, conv), (lat_hbm, lat_ref),
        ))
    ]
    for load in loads:
        load.start()
    columns = pl.ds(pl.multiple_of(section * half, LANES), half)

    def stream(j, p):
        part = pl.ds(pl.multiple_of(p * step, step), step)
        return pltpu.make_async_copy(
            qkv_hbm.at[j, part, columns], qkv.at[j, part, :], qkv_sem.at[j * pieces + p]
        )


    barrier = pltpu.get_barrier_semaphore()
    for d in range(shards):
        pl.semaphore_signal(
            barrier, inc=1,
            device_id={"section": other, "ctx": lax.rem(ctx + d, shards)}, device_id_type=MESH,
        )

    loads[0].wait()
    loads[1].wait()
    tile = 512

    def scale_part(k, carry):
        part = pl.ds(pl.multiple_of(k * tile, tile), tile)
        full = embed[:, part].astype(F32) * gain_ref[:, part]
        top = full.astype(BF16)
        scaled[:latent, part] = top
        if split:
            scaled[latent:, part] = (full - top.astype(F32)).astype(BF16)
        return carry

    lax.fori_loop(0, depth // tile, scale_part, 0)

    for load in loads[2:]:
        load.wait()
    for j in range(3):
        for p in range(pieces):
            stream(j, p).start()
    first = section == 0
    dest = jnp.where(first, dest_ref[0], dest_ref[1])
    pick = jnp.where(first, pick_ref[0:1, :], pick_ref[1:2, :])
    tier = (pick >= 4).astype(jnp.int32) + (pick >= 6).astype(jnp.int32)
    label = dest // GROUP + shards // GROUP * tier + 1
    padded = -(-shards // 8) * 8
    onehot = (iota((padded, row_count), 0) == dest).astype(F32)
    earlier = (iota((row_count, row_count), 0) < iota((row_count, row_count), 1)).astype(F32)
    before = dot(onehot.astype(BF16), earlier.astype(BF16))
    within = jnp.sum(before * onehot, axis=0, keepdims=True)
    line = iota((META, row_count), 0)
    meta = jnp.where(line == 0, dest.astype(F32), 0.0)
    meta = jnp.where(line == 1, within, meta)
    meta = jnp.where(line == 2, label.astype(F32), meta)
    outgoing[row_count:, :] = meta.astype(BF16)

    cells = frames.shape[0]
    frame = cells // frame_count
    hidden[...] = dot(frames[...], conv[0])
    hidden[frame:, :] += dot(frames[: cells - frame, :], conv[1])
    hidden[2 * frame :, :] += dot(frames[: cells - 2 * frame, :], conv[2])
    value = hidden[...]
    active = (value * jax.nn.sigmoid(value)).astype(BF16)
    channels = lat_ref.shape[0]
    per = latent // channels
    narrow = dot_nt(active, lat_ref[...]).astype(BF16)
    lane = iota((channels, LANES), 1)
    spread = ((lane % channels == iota((channels, LANES), 0)) & (lane < latent)).astype(F32)
    wide = dot(narrow, spread.astype(BF16))
    wide = jnp.where(
        iota((cells, LANES), 1) // channels == iota((cells, LANES), 0) % per, wide, 0.0
    ).astype(BF16)
    gather = (iota((row_count, cells), 1) // per == iota((row_count, cells), 0)).astype(F32)
    patches = dot(gather.astype(BF16), wide)
    narrow_patches = patches[:, :latent].astype(BF16)

    def norm_part(k, square):
        x = dot(narrow_patches, embed[:, pl.ds(pl.multiple_of(k * tile, tile), tile)])
        x = x * x
        for i in range(tile // LANES):
            square = square + x[:, i * LANES : (i + 1) * LANES]
        return square

    square = lax.fori_loop(0, depth // tile, norm_part, jnp.zeros((row_count, LANES), F32))
    scale = lax.rsqrt(jnp.sum(square, axis=1, keepdims=True) / depth + EPS)
    high = scale.astype(BF16).astype(F32)
    middle = (scale - high).astype(BF16).astype(F32)
    low = scale - high - middle
    lane = iota((row_count, LANES), 1)
    line = iota((row_count, LANES), 0)
    placed = jnp.where(line == latent + 3, label, 0).astype(F32).astype(BF16)
    message = patches + dot_nt((line == lane).astype(F32).astype(BF16), placed)
    message = jnp.where(lane == latent, high, message)
    message = jnp.where(lane == latent + 1, middle, message)
    message = jnp.where(lane == latent + 2, low, message)
    outgoing[:row_count, :] = message.astype(BF16)

    pl.semaphore_wait(barrier, shards)
    sends = []
    for d in range(shards):
        send = pltpu.make_async_remote_copy(
            src_ref=outgoing, dst_ref=rows_out.at[ctx],
            send_sem=row_send.at[d], recv_sem=row_recv.at[d],
            device_id={"section": other, "ctx": lax.rem(ctx + d, shards)}, device_id_type=MESH,
        )
        send.start()
        sends.append(send)

    def swap(j):
        return pltpu.make_async_remote_copy(
            src_ref=mine.at[j], dst_ref=weff_out.at[section, j],
            send_sem=half_send.at[j], recv_sem=half_recv.at[j],
            device_id={"section": other}, device_id_type=MESH,
        )

    def keep(j):
        return pltpu.make_async_copy(mine.at[j], weff_out.at[section, j], keep_sem.at[j])

    def contract(j, carry):
        total[...] = jnp.zeros_like(total)

        def piece(p, inner):
            stream(j, p).wait()
            part = pl.ds(pl.multiple_of(p * step, step), step)
            total[...] += dot(scaled[:, part], qkv[j, part, :])
            return inner

        lax.fori_loop(0, pieces, piece, 0)
        full = total[...]
        if split:
            full = full[:latent] + full[latent:]
        mine[j] = full.astype(BF16)
        swap(j).start()
        keep(j).start()
        return carry

    lax.fori_loop(0, 3, contract, 0)
    for send in sends:
        send.wait()
    for j in range(3):
        keep(j).wait()
        swap(j).wait()


def attend_kernel(shards, capacity, rows_ref, weff_ref, out_ref, picked_ref, row_ref, mask_ref):
    ctx = lax.axis_index("ctx")
    row_count = rows_ref.shape[1] - META
    latent = weff_ref.shape[2]
    half = weff_ref.shape[3]
    slots = out_ref.shape[0]
    total_rows = shards * row_count

    @pl.when(pl.program_id(0) == 0)
    def _():
        labels, spots = [], []
        for source in range(shards):
            meta = rows_ref[source, row_count:, :].astype(F32)
            labels.append(meta[2:3, :])
            home = meta[1:2, :] + (source * capacity)
            spots.append(jnp.where(meta[0:1, :] == ctx.astype(F32), home, -1.0))
            row_ref[source * row_count : (source + 1) * row_count, :] = rows_ref[source, :row_count, :]
        label = jnp.concatenate(labels, axis=1)
        spot = jnp.concatenate(spots, axis=1).astype(jnp.int32)
        taken = spot == iota((slots, total_rows), 0)
        picked_ref[...] = dot(taken.astype(F32).astype(BF16), row_ref[...]).astype(BF16)
        own = jnp.sum(jnp.where(taken, label, 0.0), axis=1, keepdims=True)
        mask_ref[...] = (label == own).astype(F32)

    def scale_of(block):
        return (
            block[:, latent : latent + 1].astype(F32)
            + block[:, latent + 1 : latent + 2].astype(F32)
            + block[:, latent + 2 : latent + 3].astype(F32)
        )

    def head_norm(x):
        return x * lax.rsqrt(jnp.mean(x * x, axis=-1, keepdims=True) + EPS)

    picked = picked_ref[...]
    everything = row_ref[...]
    picked_scale = scale_of(picked)
    row_scale = scale_of(everything)
    q = dot(picked[:, :latent], weff_ref[0, 0])
    k = dot(everything[:, :latent], weff_ref[0, 1])
    v = dot(everything[:, :latent], weff_ref[0, 2])
    allowed = mask_ref[...] > 0.5
    factor = 1.0 / HEAD**0.5
    for h in range(half // HEAD):
        part = slice(h * HEAD, (h + 1) * HEAD)
        queries = head_norm(q[:, part] * picked_scale).astype(BF16)
        keys = head_norm(k[:, part] * row_scale).astype(BF16)
        values = (v[:, part] * row_scale).astype(BF16)
        scores = dot_nt(queries, keys) * factor
        expo = jnp.where(allowed, jnp.exp(scores), 0.0)
        den = jnp.sum(expo, axis=1, keepdims=True)
        summed = dot(expo.astype(BF16), values)
        out_ref[:, part] = (summed / jnp.where(den > 0.0, den, 1.0)).astype(BF16)


def on_device(shards, sections, frames, w_conv, w_lat, dest, pick, w_embed, gain, w_qkv):
    _, frame_count, frame, channels = frames.shape
    latent, depth = w_embed.shape
    cells = frame_count * frame
    row_count = dest.shape[1]
    columns = w_qkv.shape[2]
    half = columns // sections
    pieces = 4
    split = SPLIT
    capacity = max(2, 3 * row_count // (2 * shards))
    slots = shards * capacity
    rows, weff = pl.pallas_call(
        functools.partial(encode_kernel, shards, frame_count, pieces, split),
        out_shape=(
            jax.ShapeDtypeStruct((shards, row_count + META, LANES), BF16),
            jax.ShapeDtypeStruct((sections, 3, latent, half), BF16),
        ),
        in_specs=[HBM] * 8,
        out_specs=(HBM, HBM),
        scratch_shapes=[
            pltpu.VMEM((cells, channels), BF16),
            pltpu.VMEM(w_conv.shape, BF16),
            pltpu.VMEM((w_lat.shape[1], channels), BF16),
            pltpu.VMEM((sections, 1, row_count), jnp.int32),
            pltpu.VMEM((sections, row_count), jnp.int32),
            pltpu.VMEM((latent, depth), BF16),
            pltpu.VMEM((1, depth), F32),
            pltpu.VMEM((3, depth, half), BF16),
            pltpu.VMEM((2 * latent if split else latent, depth), BF16),
            pltpu.VMEM((cells, channels), F32),
            pltpu.VMEM((row_count + META, LANES), BF16),
            pltpu.VMEM((3, latent, half), BF16),
            pltpu.VMEM((2 * latent if split else latent, half), F32),
            pltpu.SemaphoreType.DMA((7,)),
            pltpu.SemaphoreType.DMA((3 * pieces,)),
            pltpu.SemaphoreType.DMA((shards,)),
            pltpu.SemaphoreType.DMA((shards,)),
            pltpu.SemaphoreType.DMA((3,)),
            pltpu.SemaphoreType.DMA((3,)),
            pltpu.SemaphoreType.DMA((3,)),
        ],
        compiler_params=pltpu.CompilerParams(
            collective_id=0, has_side_effects=True, vmem_limit_bytes=67043328
        ),
    )(
        frames.reshape(cells, channels),
        w_conv,
        w_lat.T,
        dest.transpose(0, 2, 1),
        pick,
        w_embed,
        gain.reshape(1, depth),
        w_qkv.transpose(1, 0, 2),
    )
    out = pl.pallas_call(
        functools.partial(attend_kernel, shards, capacity),
        grid=(sections,),
        out_shape=jax.ShapeDtypeStruct((slots, columns), BF16),
        in_specs=[
            pl.BlockSpec((shards, row_count + META, LANES), lambda i: (0, 0, 0)),
            pl.BlockSpec((1, 3, latent, half), lambda i: (i, 0, 0, 0)),
        ],
        out_specs=pl.BlockSpec((slots, half), lambda i: (0, i)),
        scratch_shapes=[
            pltpu.VMEM((slots, LANES), BF16),
            pltpu.VMEM((shards * row_count, LANES), BF16),
            pltpu.VMEM((slots, shards * row_count), F32),
        ],
        compiler_params=pltpu.CompilerParams(vmem_limit_bytes=67043328),
    )(rows, weff)
    return out.reshape(1, slots, columns)


def solution(mesh):
    in_specs = (
        P("section", "ctx", None, None),
        P(),
        P(),
        P(None, "ctx", None),
        P(None, "ctx"),
        P(),
        P(),
        P(None, None, "mp"),
    )
    return jax.shard_map(
        functools.partial(on_device, mesh.shape["ctx"], mesh.shape["section"]),
        mesh=mesh,
        in_specs=in_specs,
        out_specs=P("section", "ctx", "mp"),
        check_vma=False,
    )
```
